32 devices in a mesh: energy: 8 (over y, x, core), slab: 4 (over z).
Axes of the slice: x: 2, y: 2, z: 4, core: 2. Of those that a mesh axis runs over, the one named last changes fastest.
Arguments:
- green: bfloat16 [32, 8, 2, 128, 128], P('energy', 'slab'), may hold values from -6 to 6
- coupling: bfloat16 [8, 6, 2, 128, 128], P('slab'), may hold values from -0.1875 to 0.1875
- neighbours: int32 [8, 6], P('slab'), may hold values from 0 to 7, as said below
- shifts: int32 [2], replicated, may hold values from 1 to 4, as said below
- occupation: float32 [2], replicated, may hold values from 0.3 to 3
Outputs:
- self_energy: bfloat16 [32, 8, 2, 128, 128], P('energy', 'slab')
The draws below stay inside these ranges and needn't reach their ends.
Inputs may be any that keep to these rules, and one draw needn't show every extreme that they name: `neighbours`: each entry differs from its own atom's index by 1 to 2; column 0 differs by exactly 2. `shifts`: exactly one mode has shift 4; the others are below it.
All inputs are finite; a program needn't handle non-finite values.
Results may differ from the reference program's by a relative error of at most 0.0057.
Values may be sent and summed in bfloat16 or wider, within the bound.
A program may use at most 128 MiB of HBM per device.

```python
import math
import jax
import jax.numpy as jnp
from jax import lax

BLK = 128
NBR = 6
NMODE = 2
WID = 4
HALO = 2
NE = 32
NA = 8


def draw_neighbours(key, part):
    key_mag, key_sign = jax.random.split(jax.random.fold_in(key, 11), 2)
    magnitude = jax.random.randint(key_mag, (NA, NBR), 1, HALO + 1)
    magnitude = magnitude.at[:, 0].set(HALO)
    signs = 2 * jax.random.randint(key_sign, (NA, NBR), 0, 2) - 1
    atom_ids = jnp.arange(NA, dtype=jnp.int32)[:, None]
    forward = atom_ids + signs * magnitude
    backward = atom_ids - signs * magnitude
    inside = (forward >= 0) & (forward < NA)
    return jnp.where(inside, forward, backward).astype(jnp.int32)


def draw_shifts(key, part):
    key_vals, key_pick = jax.random.split(jax.random.fold_in(key, 23), 2)
    values = jax.random.randint(key_vals, (NMODE,), 1, WID)
    chosen = jax.random.randint(key_pick, (), 0, NMODE)
    return jnp.where(jnp.arange(NMODE) == chosen, WID, values).astype(jnp.int32)


def shard_levels(rng, dims, pieces, smallest, largest):
    factor_of, own = 1.0, jax.random.fold_in(rng, 6)
    for dim, blocks in pieces:
        heights = jnp.exp(jax.random.uniform(jax.random.fold_in(own, dim), (blocks,), jnp.float32, smallest / len(pieces), largest / len(pieces)))
        factor_of = factor_of * jnp.repeat(heights, dims[dim] // blocks).reshape([-1 if axis == dim else 1 for axis in range(len(dims))])
    return factor_of


def bell_draw(stream_key, shape, width, bound, cuts=(), kind=jnp.bfloat16):
    loudness = shard_levels(stream_key, shape, cuts, -0.22, 0.18) if cuts else 1.0
    array = jax.random.normal(stream_key, shape, jnp.float32) * width * loudness
    return jnp.minimum(jnp.maximum(array, -bound), bound).astype(kind)


def setup_inputs(seed: int = 0) -> dict:
    keys = jax.random.split(jax.random.key(seed), 6)
    green = bell_draw(keys[0], (NE, NA, 2, BLK, BLK), 1.0, 6.0, ((0, 8), (1, 4)))
    coupling = bell_draw(keys[1], (NA, NBR, NMODE, BLK, BLK), (BLK * 8) ** -0.5, 0.1875, ((0, 4),))
    neighbours = draw_neighbours(jax.random.fold_in(keys[5], 71), 0)
    shifts = draw_shifts(jax.random.fold_in(keys[5], 71), 0)
    occupation = jnp.clip(jnp.exp(jax.random.uniform(keys[4], (NMODE,), jnp.float32, math.log(0.3), math.log(3.0))), 0.3, 3.0)
    return {"green": green, "coupling": coupling, "neighbours": neighbours, "shifts": shifts, "occupation": occupation}


def atom_terms(green, coupling_row, neighbour_row, shifts, occupation):
    result = jnp.zeros((NE, 2, BLK, BLK), jnp.float32)
    for which_mode in range(NMODE):
        running = jnp.zeros((NE, 2, BLK, BLK), jnp.float32)
        for which_slot in range(NBR):
            source = lax.dynamic_index_in_dim(green, neighbour_row[which_slot].astype(jnp.int32), 1, keepdims=False).astype(jnp.float32)
            matrix = coupling_row[which_slot, which_mode].astype(jnp.float32)
            half_product = jnp.einsum("ik,erkl->eril", matrix, source).astype(jnp.bfloat16).astype(jnp.float32)
            running = running + jnp.einsum("eril,jl->erij", half_product, matrix)
        product = running.astype(jnp.bfloat16)
        padded = jnp.pad(product, ((WID, WID), (0, 0), (0, 0), (0, 0)))
        step_size = shifts[which_mode].astype(jnp.int32)
        lower = lax.dynamic_slice_in_dim(padded, (WID - step_size).astype(jnp.int32), NE, 0).astype(jnp.float32)
        upper = lax.dynamic_slice_in_dim(padded, (WID + step_size).astype(jnp.int32), NE, 0).astype(jnp.float32)
        weight = occupation[which_mode]
        result = result + (weight + 1.0) * lower + weight * upper
    return result.astype(jnp.bfloat16)


def reference(green, coupling, neighbours, shifts, occupation):
    per_atom = lax.map(lambda pair: atom_terms(green, pair[0], pair[1], shifts, occupation), (coupling, neighbours))
    return jnp.transpose(per_atom, (1, 0, 2, 3, 4))
```

```python
import functools

import jax
import jax.numpy as jnp
from jax import lax
from jax.experimental import pallas as pl
from jax.experimental.pallas import tpu as pltpu
from jax.sharding import PartitionSpec as P

WID = 4
HALO = 2
MESH = pl.DeviceIdType.MESH


def energy_order(count):
    order = []
    for low in range((count + 1) // 2):
        order.append(low)
        if count - 1 - low != low:
            order.append(count - 1 - low)
    return order


def kernel(sizes, nbr, shifts, occ, green, coupling, out, *scratch):
    energies, atoms, parts, blk, slots, modes, n_energy, n_slab = sizes
    wide = scratch[:energies]
    (coup, prod, low_send, up_send, low_recv, up_recv, own, result,
     coup_sem, local_sem, slab_send, slab_recv, en_send, en_recv, out_sem) = scratch[energies:]
    me_e = lax.axis_index("energy")
    me_s = lax.axis_index("slab")
    has_prev, has_next = me_e > 0, me_e < n_energy - 1
    has_left, has_right = me_s > 0, me_s < n_slab - 1
    order = energy_order(energies)

    coup_copy = pltpu.make_async_copy(coupling, coup, coup_sem)
    local = [
        pltpu.make_async_copy(green.at[e], wide[e].at[HALO : HALO + atoms], local_sem.at[e])
        for e in range(energies)
    ]
    for e in order:
        local[e].start()
    coup_copy.start()

    barrier = pltpu.get_barrier_semaphore()
    sides = (
        (has_left, {"slab": me_s - 1}),
        (has_right, {"slab": me_s + 1}),
        (has_prev, {"energy": me_e - 1}),
        (has_next, {"energy": me_e + 1}),
    )
    for there, device in sides:
        @pl.when(there)
        def _(device=device):
            pl.semaphore_signal(barrier, inc=1, device_id=device, device_id_type=MESH)
    peers = sum(there.astype(jnp.int32) for there, _ in sides)
    pl.semaphore_wait(barrier, peers)

    def slab_copy(e, direction):
        if direction == 0:
            src, dst, to = green.at[e, atoms - HALO : atoms], wide[e].at[0:HALO], me_s + 1
        else:
            src, dst, to = green.at[e, 0:HALO], wide[e].at[HALO + atoms : 2 * HALO + atoms], me_s - 1
        return pltpu.make_async_remote_copy(
            src_ref=src,
            dst_ref=dst,
            send_sem=slab_send.at[direction, e],
            recv_sem=slab_recv.at[direction, e],
            device_id={"slab": to},
            device_id_type=MESH,
        )

    for e in order:
        @pl.when(has_right)
        def _(e=e):
            slab_copy(e, 0).start()
        @pl.when(has_left)
        def _(e=e):
            slab_copy(e, 1).start()

    def energy_copy(u, direction):
        if direction == 0:
            src, dst, to = low_send.at[u], low_recv.at[u], me_e + 1
        else:
            src, dst, to = up_send.at[u], up_recv.at[u], me_e - 1
        return pltpu.make_async_remote_copy(
            src_ref=src,
            dst_ref=dst,
            send_sem=en_send.at[direction, u],
            recv_sem=en_recv.at[direction, u],
            device_id={"energy": to},
            device_id_type=MESH,
        )

    @pl.when(jnp.logical_not(has_prev))
    def _():
        low_recv[...] = jnp.zeros_like(low_recv)
    @pl.when(jnp.logical_not(has_next))
    def _():
        up_recv[...] = jnp.zeros_like(up_recv)

    first_atom = me_s * atoms

    def products(e):
        def body(a, carry):
            halves, mats = [], []
            for j in range(slots):
                g = wide[e][jnp.clip(nbr[a, j] - first_atom + HALO, 0, atoms + 2 * HALO - 1)]
                g = jnp.concatenate([g[r] for r in range(parts)], axis=1)
                c = coup[a, j]
                mats.append(c)
                h = jnp.dot(c.reshape(modes * blk, blk), g, preferred_element_type=jnp.float32)
                halves.append(h.astype(jnp.bfloat16))
            for m in range(modes):
                rows = [
                    jnp.concatenate(
                        [h[m * blk : (m + 1) * blk, r * blk : (r + 1) * blk] for h in halves], axis=1
                    )
                    for r in range(parts)
                ]
                lhs = jnp.concatenate(rows, axis=0)
                rhs = jnp.concatenate([c[m] for c in mats], axis=1)
                p = lax.dot_general(lhs, rhs, (((1,), (1,)), ((), ())), preferred_element_type=jnp.float32)
                prod[m, e, a] = p.reshape(parts, blk, blk).astype(jnp.bfloat16)
            return carry

        lax.fori_loop(0, atoms, body, 0)

    def gathered(terms):
        def at(a):
            total = None
            for m, index, weight in terms:
                inside = (index >= 0) & (index < energies)
                safe = jnp.clip(index, 0, energies - 1)
                term = jnp.where(inside, weight, 0.0) * prod[m, safe, a].astype(jnp.float32)
                total = term if total is None else total + term
            return total

        return at

    def store_sum(target, u, terms):
        at = gathered(terms)

        def body(a, carry):
            target[u, a] = at(a).astype(target.dtype)
            return carry

        lax.fori_loop(0, atoms, body, 0)

    done, sent = set(), set()
    for e in order:
        local[e].wait()
        if not done:
            coup_copy.wait()
        @pl.when(has_left)
        def _(e=e):
            slab_copy(e, 0).wait_recv()
        @pl.when(has_right)
        def _(e=e):
            slab_copy(e, 1).wait_recv()
        products(e)
        done.add(e)
        for u in range(WID):
            if ("up", u) not in sent and set(range(u + 1)) <= done:
                sent.add(("up", u))
                @pl.when(has_prev)
                def _(u=u):
                    store_sum(up_send, u, [(m, u - WID + shifts[m], occ[m]) for m in range(modes)])
                    energy_copy(u, 1).start()
        for u in reversed(range(WID)):
            if ("low", u) not in sent and set(range(energies - WID + u, energies)) <= done:
                sent.add(("low", u))
                @pl.when(has_next)
                def _(u=u):
                    store_sum(low_send, u, [(m, energies + u - shifts[m], occ[m] + 1.0) for m in range(modes)])
                    energy_copy(u, 0).start()

    for t in range(energies):
        terms = []
        for m in range(modes):
            terms.append((m, t - shifts[m], occ[m] + 1.0))
            terms.append((m, t + shifts[m], occ[m]))
        store_sum(own, t, terms)

    for t in order:
        low_u = t if t < WID else None
        up_u = t - (energies - WID) if t >= energies - WID else None
        if low_u is not None:
            @pl.when(has_prev)
            def _(u=low_u):
                energy_copy(u, 0).wait_recv()
        if up_u is not None:
            @pl.when(has_next)
            def _(u=up_u):
                energy_copy(u, 1).wait_recv()

        def body(a, carry, t=t, low_u=low_u, up_u=up_u):
            total = own[t, a]
            if low_u is not None:
                total = total + low_recv[low_u, a].astype(jnp.float32)
            if up_u is not None:
                total = total + up_recv[up_u, a].astype(jnp.float32)
            result[t, a] = total.astype(jnp.bfloat16)
            return carry

        lax.fori_loop(0, atoms, body, 0)
        pltpu.make_async_copy(result.at[t], out.at[t], out_sem.at[t]).start()

    for e in order:
        @pl.when(has_right)
        def _(e=e):
            slab_copy(e, 0).wait_send()
        @pl.when(has_left)
        def _(e=e):
            slab_copy(e, 1).wait_send()
    for u in range(WID):
        @pl.when(has_next)
        def _(u=u):
            energy_copy(u, 0).wait_send()
        @pl.when(has_prev)
        def _(u=u):
            energy_copy(u, 1).wait_send()
    for t in order:
        pltpu.make_async_copy(result.at[t], out.at[t], out_sem.at[t]).wait()


def solution(mesh):
    def shards(green, coupling, neighbours, shifts, occupation):
        energies, atoms, parts, blk, _ = green.shape
        slots, modes = coupling.shape[1:3]
        sizes = (energies, atoms, parts, blk, slots, modes, mesh.shape["energy"], mesh.shape["slab"])
        bf16, f32 = jnp.bfloat16, jnp.float32
        smem = pl.BlockSpec(memory_space=pltpu.SMEM)
        hbm = pl.BlockSpec(memory_space=pl.ANY)
        edge = (WID, atoms, parts, blk, blk)
        dma = pltpu.SemaphoreType.DMA
        return pl.pallas_call(
            functools.partial(kernel, sizes),
            out_shape=jax.ShapeDtypeStruct(green.shape, bf16),
            in_specs=[smem, smem, smem, hbm, hbm],
            out_specs=hbm,
            scratch_shapes=[pltpu.VMEM((atoms + 2 * HALO, parts, blk, blk), bf16) for _ in range(energies)]
            + [
                pltpu.VMEM(coupling.shape, bf16),
                pltpu.VMEM((modes, energies, atoms, parts, blk, blk), bf16),
                pltpu.VMEM(edge, bf16),
                pltpu.VMEM(edge, bf16),
                pltpu.VMEM(edge, bf16),
                pltpu.VMEM(edge, bf16),
                pltpu.VMEM(green.shape, f32),
                pltpu.VMEM(green.shape, bf16),
                dma,
                dma((energies,)),
                dma((2, energies)),
                dma((2, energies)),
                dma((2, WID)),
                dma((2, WID)),
                dma((energies,)),
            ],
            compiler_params=pltpu.CompilerParams(collective_id=0, has_side_effects=True),
        )(neighbours, shifts, occupation, green, coupling)

    return jax.shard_map(
        shards,
        mesh=mesh,
        in_specs=(
            P("energy", "slab", None, None, None),
            P("slab", None, None, None, None),
            P("slab", None),
            P(),
            P(),
        ),
        out_specs=P("energy", "slab", None, None, None),
        check_vma=False,
    )
```

```python
import functools

import jax
import jax.numpy as jnp
from jax import lax
from jax.experimental import pallas as pl
from jax.experimental.pallas import tpu as pltpu
from jax.sharding import PartitionSpec as P

WID = 4
HALO = 2
MESH = pl.DeviceIdType.MESH


def energy_order(count):
    order = []
    for low in range((count + 1) // 2):
        order.append(low)
        if count - 1 - low != low:
            order.append(count - 1 - low)
    return order


def kernel(sizes, nbr, shifts, occ, green, coupling, out, *scratch):
    energies, atoms, parts, blk, slots, modes, n_energy, n_slab = sizes
    wide = [scratch[r * energies : (r + 1) * energies] for r in range(parts)]
    (coup, prod, low_send, up_send, low_recv, up_recv, own,
     coup_sem, local_sem, slab_send, slab_recv, en_send, en_recv) = scratch[parts * energies :]
    me_e = lax.axis_index("energy")
    me_s = lax.axis_index("slab")
    has_prev, has_next = me_e > 0, me_e < n_energy - 1
    has_left, has_right = me_s > 0, me_s < n_slab - 1
    order = energy_order(energies)

    coup_copy = pltpu.make_async_copy(coupling, coup, coup_sem)
    local = [
        [
            pltpu.make_async_copy(green.at[e, :, r], wide[r][e].at[HALO : HALO + atoms], local_sem.at[r, e])
            for e in range(energies)
        ]
        for r in range(parts)
    ]
    for r in range(parts):
        for e in order:
            local[r][e].start()
    coup_copy.start()

    barrier = pltpu.get_barrier_semaphore()
    sides = (
        (has_left, {"slab": me_s - 1}),
        (has_right, {"slab": me_s + 1}),
        (has_prev, {"energy": me_e - 1}),
        (has_next, {"energy": me_e + 1}),
    )
    for there, device in sides:
        @pl.when(there)
        def _(device=device):
            pl.semaphore_signal(barrier, inc=1, device_id=device, device_id_type=MESH)
    peers = sum(there.astype(jnp.int32) for there, _ in sides)
    pl.semaphore_wait(barrier, peers)

    def slab_copy(r, e, direction):
        halo = wide[r][e]
        if direction == 0:
            src, dst, to = green.at[e, atoms - HALO : atoms, r], halo.at[0:HALO], me_s + 1
        else:
            src, dst, to = green.at[e, 0:HALO, r], halo.at[HALO + atoms : 2 * HALO + atoms], me_s - 1
        return pltpu.make_async_remote_copy(
            src_ref=src,
            dst_ref=dst,
            send_sem=slab_send.at[direction, r, e],
            recv_sem=slab_recv.at[direction, r, e],
            device_id={"slab": to},
            device_id_type=MESH,
        )

    for r in range(parts):
        for e in order:
            @pl.when(has_right)
            def _(e=e, r=r):
                slab_copy(r, e, 0).start()
            @pl.when(has_left)
            def _(e=e, r=r):
                slab_copy(r, e, 1).start()

    def energy_copy(r, u, direction):
        if direction == 0:
            src, dst, to = low_send.at[r, u], low_recv.at[r, u], me_e + 1
        else:
            src, dst, to = up_send.at[r, u], up_recv.at[r, u], me_e - 1
        return pltpu.make_async_remote_copy(
            src_ref=src,
            dst_ref=dst,
            send_sem=en_send.at[direction, r, u],
            recv_sem=en_recv.at[direction, r, u],
            device_id={"energy": to},
            device_id_type=MESH,
        )

    @pl.when(jnp.logical_not(has_prev))
    def _():
        low_recv[...] = jnp.zeros_like(low_recv)
    @pl.when(jnp.logical_not(has_next))
    def _():
        up_recv[...] = jnp.zeros_like(up_recv)

    first_atom = me_s * atoms

    def products(r, e):
        def body(a, carry):
            halves, mats = [], []
            for j in range(slots):
                g = wide[r][e][jnp.clip(nbr[a, j] - first_atom + HALO, 0, atoms + 2 * HALO - 1)]
                c = coup[a, j]
                mats.append(c)
                h = jnp.dot(c.reshape(modes * blk, blk), g, preferred_element_type=jnp.float32)
                halves.append(h.astype(jnp.bfloat16))
            for m in range(modes):
                lhs = jnp.concatenate([h[m * blk : (m + 1) * blk] for h in halves], axis=1)
                rhs = jnp.concatenate([c[m] for c in mats], axis=1)
                p = lax.dot_general(lhs, rhs, (((1,), (1,)), ((), ())), preferred_element_type=jnp.float32)
                prod[m, r, e, a] = p.astype(jnp.bfloat16)
            return carry

        lax.fori_loop(0, atoms, body, 0)

    def store_sum(target, r, u, terms):
        def body(a, carry):
            total = None
            for m, index, weight in terms:
                inside = (index >= 0) & (index < energies)
                safe = jnp.clip(index, 0, energies - 1)
                term = jnp.where(inside, weight, 0.0) * prod[m, r, safe, a].astype(jnp.float32)
                total = term if total is None else total + term
            target[r, u, a] = total.astype(target.dtype)
            return carry

        lax.fori_loop(0, atoms, body, 0)

    for r in range(parts):
        done, sent = set(), set()
        for e in order:
            local[r][e].wait()
            if r == 0 and not done:
                coup_copy.wait()
            @pl.when(has_left)
            def _(e=e, r=r):
                slab_copy(r, e, 0).wait_recv()
            @pl.when(has_right)
            def _(e=e, r=r):
                slab_copy(r, e, 1).wait_recv()
            products(r, e)
            done.add(e)
            for u in range(WID):
                if ("up", u) not in sent and set(range(u + 1)) <= done:
                    sent.add(("up", u))
                    @pl.when(has_prev)
                    def _(u=u, r=r):
                        store_sum(up_send, r, u, [(m, u - WID + shifts[m], occ[m]) for m in range(modes)])
                        energy_copy(r, u, 1).start()
            for u in reversed(range(WID)):
                if ("low", u) not in sent and set(range(energies - WID + u, energies)) <= done:
                    sent.add(("low", u))
                    @pl.when(has_next)
                    def _(u=u, r=r):
                        store_sum(
                            low_send, r, u, [(m, energies + u - shifts[m], occ[m] + 1.0) for m in range(modes)]
                        )
                        energy_copy(r, u, 0).start()

    for r in range(parts):
        for t in range(energies):
            terms = []
            for m in range(modes):
                terms.append((m, t - shifts[m], occ[m] + 1.0))
                terms.append((m, t + shifts[m], occ[m]))
            store_sum(own, r, t, terms)

    for r in range(parts):
        for t in order:
            low_u = t if t < WID else None
            up_u = t - (energies - WID) if t >= energies - WID else None
            if low_u is not None:
                @pl.when(has_prev)
                def _(u=low_u, r=r):
                    energy_copy(r, u, 0).wait_recv()
            if up_u is not None:
                @pl.when(has_next)
                def _(u=up_u, r=r):
                    energy_copy(r, u, 1).wait_recv()

            def body(a, carry, t=t, r=r, low_u=low_u, up_u=up_u):
                total = own[r, t, a]
                if low_u is not None:
                    total = total + low_recv[r, low_u, a].astype(jnp.float32)
                if up_u is not None:
                    total = total + up_recv[r, up_u, a].astype(jnp.float32)
                out[t, a, r] = total.astype(jnp.bfloat16)
                return carry

            lax.fori_loop(0, atoms, body, 0)

    for r in range(parts):
        for e in order:
            @pl.when(has_right)
            def _(e=e, r=r):
                slab_copy(r, e, 0).wait_send()
            @pl.when(has_left)
            def _(e=e, r=r):
                slab_copy(r, e, 1).wait_send()
        for u in range(WID):
            @pl.when(has_next)
            def _(u=u, r=r):
                energy_copy(r, u, 0).wait_send()
            @pl.when(has_prev)
            def _(u=u, r=r):
                energy_copy(r, u, 1).wait_send()


def solution(mesh):
    def shards(green, coupling, neighbours, shifts, occupation):
        energies, atoms, parts, blk, _ = green.shape
        slots, modes = coupling.shape[1:3]
        sizes = (energies, atoms, parts, blk, slots, modes, mesh.shape["energy"], mesh.shape["slab"])
        bf16, f32 = jnp.bfloat16, jnp.float32
        smem = pl.BlockSpec(memory_space=pltpu.SMEM)
        hbm = pl.BlockSpec(memory_space=pl.ANY)
        edge = (parts, WID, atoms, blk, blk)
        dma = pltpu.SemaphoreType.DMA
        return pl.pallas_call(
            functools.partial(kernel, sizes),
            out_shape=jax.ShapeDtypeStruct(green.shape, bf16),
            in_specs=[smem, smem, smem, hbm, hbm],
            out_specs=pl.BlockSpec(memory_space=pltpu.VMEM),
            scratch_shapes=[pltpu.VMEM((atoms + 2 * HALO, blk, blk), bf16) for _ in range(parts * energies)]
            + [
                pltpu.VMEM(coupling.shape, bf16),
                pltpu.VMEM((modes, parts, energies, atoms, blk, blk), bf16),
                pltpu.VMEM(edge, bf16),
                pltpu.VMEM(edge, bf16),
                pltpu.VMEM(edge, bf16),
                pltpu.VMEM(edge, bf16),
                pltpu.VMEM((parts, energies, atoms, blk, blk), f32),
                dma,
                dma((parts, energies)),
                dma((2, parts, energies)),
                dma((2, parts, energies)),
                dma((2, parts, WID)),
                dma((2, parts, WID)),
            ],
            compiler_params=pltpu.CompilerParams(collective_id=0, has_side_effects=True),
        )(neighbours, shifts, occupation, green, coupling)

    return jax.shard_map(
        shards,
        mesh=mesh,
        in_specs=(
            P("energy", "slab", None, None, None),
            P("slab", None, None, None, None),
            P("slab", None),
            P(),
            P(),
        ),
        out_specs=P("energy", "slab", None, None, None),
        check_vma=False,
    )
```

```python
import functools

import jax
import jax.numpy as jnp
from jax import lax
from jax.experimental import pallas as pl
from jax.experimental.pallas import tpu as pltpu
from jax.sharding import PartitionSpec as P

WID = 4
HALO = 2
MESH = pl.DeviceIdType.MESH


def energy_order(count):
    order = []
    for low in range((count + 1) // 2):
        order.append(low)
        if count - 1 - low != low:
            order.append(count - 1 - low)
    return order


def kernel(sizes, nbr_hbm, shifts_hbm, occ_hbm, green, coupling, out, *scratch):
    energies, atoms, parts, blk, slots, modes, n_energy, n_slab = sizes
    wide = [scratch[r * energies : (r + 1) * energies] for r in range(parts)]
    (coup, prod, low_send, up_send, low_recv, up_recv, own, nbr, shifts, occ,
     coup_sem, local_sem, slab_send, slab_recv, en_send, en_recv, small_sem) = scratch[parts * energies :]
    me_e = lax.axis_index("energy")
    me_s = lax.axis_index("slab")
    has_prev, has_next = me_e > 0, me_e < n_energy - 1
    has_left, has_right = me_s > 0, me_s < n_slab - 1
    order = energy_order(energies)

    small = [
        pltpu.make_async_copy(src, dst, small_sem.at[k])
        for k, (src, dst) in enumerate(((nbr_hbm, nbr), (shifts_hbm, shifts), (occ_hbm, occ)))
    ]
    for copy in small:
        copy.start()
    coup_copy = pltpu.make_async_copy(coupling, coup, coup_sem)
    local = [
        [
            pltpu.make_async_copy(green.at[e, :, r], wide[r][e].at[HALO : HALO + atoms], local_sem.at[r, e])
            for e in range(energies)
        ]
        for r in range(parts)
    ]
    for r in range(parts):
        for e in order:
            local[r][e].start()
    coup_copy.start()

    barrier = pltpu.get_barrier_semaphore()
    sides = (
        (has_left, {"slab": me_s - 1}),
        (has_right, {"slab": me_s + 1}),
        (has_prev, {"energy": me_e - 1}),
        (has_next, {"energy": me_e + 1}),
    )
    for there, device in sides:
        @pl.when(there)
        def _(device=device):
            pl.semaphore_signal(barrier, inc=1, device_id=device, device_id_type=MESH)
    peers = sum(there.astype(jnp.int32) for there, _ in sides)
    pl.semaphore_wait(barrier, peers)

    def slab_copy(r, e, direction):
        halo = wide[r][e]
        if direction == 0:
            src, dst, to = green.at[e, atoms - HALO : atoms, r], halo.at[0:HALO], me_s + 1
        else:
            src, dst, to = green.at[e, 0:HALO, r], halo.at[HALO + atoms : 2 * HALO + atoms], me_s - 1
        return pltpu.make_async_remote_copy(
            src_ref=src,
            dst_ref=dst,
            send_sem=slab_send.at[direction, r, e],
            recv_sem=slab_recv.at[direction, r, e],
            device_id={"slab": to},
            device_id_type=MESH,
        )

    for r in range(parts):
        for e in order:
            @pl.when(has_right)
            def _(e=e, r=r):
                slab_copy(r, e, 0).start()
            @pl.when(has_left)
            def _(e=e, r=r):
                slab_copy(r, e, 1).start()

    def energy_copy(r, u, direction):
        if direction == 0:
            src, dst, to = low_send.at[r, u], low_recv.at[r, u], me_e + 1
        else:
            src, dst, to = up_send.at[r, u], up_recv.at[r, u], me_e - 1
        return pltpu.make_async_remote_copy(
            src_ref=src,
            dst_ref=dst,
            send_sem=en_send.at[direction, r, u],
            recv_sem=en_recv.at[direction, r, u],
            device_id={"energy": to},
            device_id_type=MESH,
        )

    @pl.when(jnp.logical_not(has_prev))
    def _():
        low_recv[...] = jnp.zeros_like(low_recv)
    @pl.when(jnp.logical_not(has_next))
    def _():
        up_recv[...] = jnp.zeros_like(up_recv)

    first_atom = me_s * atoms

    def products(r, e):
        def body(a, carry):
            halves, mats = [], []
            for j in range(slots):
                g = wide[r][e][jnp.clip(nbr[a, j] - first_atom + HALO, 0, atoms + 2 * HALO - 1)]
                c = coup[a, j]
                mats.append(c)
                h = jnp.dot(c.reshape(modes * blk, blk), g, preferred_element_type=jnp.float32)
                halves.append(h.astype(jnp.bfloat16))
            for m in range(modes):
                lhs = jnp.concatenate([h[m * blk : (m + 1) * blk] for h in halves], axis=1)
                rhs = jnp.concatenate([c[m] for c in mats], axis=1)
                p = lax.dot_general(lhs, rhs, (((1,), (1,)), ((), ())), preferred_element_type=jnp.float32)
                prod[m, r, e, a] = p.astype(jnp.bfloat16)
            return carry

        lax.fori_loop(0, atoms, body, 0)

    def store_sum(target, r, u, terms):
        def body(a, carry):
            total = None
            for m, index, weight in terms:
                inside = (index >= 0) & (index < energies)
                safe = jnp.clip(index, 0, energies - 1)
                term = jnp.where(inside, weight, 0.0) * prod[m, r, safe, a].astype(jnp.float32)
                total = term if total is None else total + term
            target[r, u, a] = total.astype(target.dtype)
            return carry

        lax.fori_loop(0, atoms, body, 0)

    for r in range(parts):
        done, sent = set(), set()
        for e in order:
            local[r][e].wait()
            if r == 0 and not done:
                coup_copy.wait()
                for copy in small:
                    copy.wait()
            @pl.when(has_left)
            def _(e=e, r=r):
                slab_copy(r, e, 0).wait_recv()
            @pl.when(has_right)
            def _(e=e, r=r):
                slab_copy(r, e, 1).wait_recv()
            products(r, e)
            done.add(e)
            for u in range(WID):
                if ("up", u) not in sent and set(range(u + 1)) <= done:
                    sent.add(("up", u))
                    @pl.when(has_prev)
                    def _(u=u, r=r):
                        store_sum(up_send, r, u, [(m, u - WID + shifts[m], occ[m]) for m in range(modes)])
                        energy_copy(r, u, 1).start()
            for u in reversed(range(WID)):
                if ("low", u) not in sent and set(range(energies - WID + u, energies)) <= done:
                    sent.add(("low", u))
                    @pl.when(has_next)
                    def _(u=u, r=r):
                        store_sum(
                            low_send, r, u, [(m, energies + u - shifts[m], occ[m] + 1.0) for m in range(modes)]
                        )
                        energy_copy(r, u, 0).start()

    for r in range(parts):
        for t in range(energies):
            terms = []
            for m in range(modes):
                terms.append((m, t - shifts[m], occ[m] + 1.0))
                terms.append((m, t + shifts[m], occ[m]))
            store_sum(own, r, t, terms)

    for r in range(parts):
        for t in order:
            low_u = t if t < WID else None
            up_u = t - (energies - WID) if t >= energies - WID else None
            if low_u is not None:
                @pl.when(has_prev)
                def _(u=low_u, r=r):
                    energy_copy(r, u, 0).wait_recv()
            if up_u is not None:
                @pl.when(has_next)
                def _(u=up_u, r=r):
                    energy_copy(r, u, 1).wait_recv()

            def body(a, carry, t=t, r=r, low_u=low_u, up_u=up_u):
                total = own[r, t, a]
                if low_u is not None:
                    total = total + low_recv[r, low_u, a].astype(jnp.float32)
                if up_u is not None:
                    total = total + up_recv[r, up_u, a].astype(jnp.float32)
                out[t, a, r] = total.astype(jnp.bfloat16)
                return carry

            lax.fori_loop(0, atoms, body, 0)

    for r in range(parts):
        for e in order:
            @pl.when(has_right)
            def _(e=e, r=r):
                slab_copy(r, e, 0).wait_send()
            @pl.when(has_left)
            def _(e=e, r=r):
                slab_copy(r, e, 1).wait_send()
        for u in range(WID):
            @pl.when(has_next)
            def _(u=u, r=r):
                energy_copy(r, u, 0).wait_send()
            @pl.when(has_prev)
            def _(u=u, r=r):
                energy_copy(r, u, 1).wait_send()


def solution(mesh):
    def shards(green, coupling, neighbours, shifts, occupation):
        energies, atoms, parts, blk, _ = green.shape
        slots, modes = coupling.shape[1:3]
        sizes = (energies, atoms, parts, blk, slots, modes, mesh.shape["energy"], mesh.shape["slab"])
        bf16, f32 = jnp.bfloat16, jnp.float32
        hbm = pl.BlockSpec(memory_space=pltpu.HBM)
        edge = (parts, WID, atoms, blk, blk)
        dma = pltpu.SemaphoreType.DMA
        return pl.pallas_call(
            functools.partial(kernel, sizes),
            out_shape=pltpu.VMEM(green.shape, bf16),
            in_specs=[hbm] * 5,
            out_specs=pl.BlockSpec(memory_space=pltpu.VMEM),
            scratch_shapes=[pltpu.VMEM((atoms + 2 * HALO, blk, blk), bf16) for _ in range(parts * energies)]
            + [
                pltpu.VMEM(coupling.shape, bf16),
                pltpu.VMEM((modes, parts, energies, atoms, blk, blk), bf16),
                pltpu.VMEM(edge, bf16),
                pltpu.VMEM(edge, bf16),
                pltpu.VMEM(edge, bf16),
                pltpu.VMEM(edge, bf16),
                pltpu.VMEM((parts, energies, atoms, blk, blk), f32),
                pltpu.SMEM((atoms, slots), jnp.int32),
                pltpu.SMEM((modes,), jnp.int32),
                pltpu.SMEM((modes,), f32),
                dma,
                dma((parts, energies)),
                dma((2, parts, energies)),
                dma((2, parts, energies)),
                dma((2, parts, WID)),
                dma((2, parts, WID)),
                dma((3,)),
            ],
            compiler_params=pltpu.CompilerParams(collective_id=0, has_side_effects=True),
        )(neighbours, shifts, occupation, green, coupling)

    return jax.shard_map(
        shards,
        mesh=mesh,
        in_specs=(
            P("energy", "slab", None, None, None),
            P("slab", None, None, None, None),
            P("slab", None),
            P(),
            P(),
        ),
        out_specs=P("energy", "slab", None, None, None),
        check_vma=False,
    )
```

```python
import functools

import jax
import jax.numpy as jnp
from jax import lax
from jax.experimental import pallas as pl
from jax.experimental.pallas import tpu as pltpu
from jax.sharding import PartitionSpec as P

WID = 4
HALO = 2
MESH = pl.DeviceIdType.MESH


def energy_order(count):
    order = []
    for low in range((count + 1) // 2):
        order.append(low)
        if count - 1 - low != low:
            order.append(count - 1 - low)
    return order


def kernel(sizes, nbr_hbm, shifts_hbm, occ_hbm, green, coupling, out, *scratch):
    energies, atoms, parts, blk, slots, modes, n_energy, n_slab = sizes
    wide = [scratch[r * energies : (r + 1) * energies] for r in range(parts)]
    (coup, prod, low_send, up_send, low_recv, up_recv, own, nbr, shifts, occ,
     coup_sem, local_sem, slab_send, slab_recv, en_send, en_recv, small_sem) = scratch[parts * energies :]
    me_e = lax.axis_index("energy")
    me_s = lax.axis_index("slab")
    has_prev, has_next = me_e > 0, me_e < n_energy - 1
    has_left, has_right = me_s > 0, me_s < n_slab - 1
    order = energy_order(energies)

    small = [
        pltpu.make_async_copy(src, dst, small_sem.at[k])
        for k, (src, dst) in enumerate(((nbr_hbm, nbr), (shifts_hbm, shifts), (occ_hbm, occ)))
    ]
    for copy in small:
        copy.start()
    coup_copy = pltpu.make_async_copy(coupling, coup, coup_sem)
    local = [
        [
            pltpu.make_async_copy(green.at[e, :, r], wide[r][e].at[HALO : HALO + atoms], local_sem.at[r, e])
            for e in range(energies)
        ]
        for r in range(parts)
    ]
    for r in range(parts):
        for e in order:
            local[r][e].start()
    coup_copy.start()

    barrier = pltpu.get_barrier_semaphore()
    sides = (
        (has_left, {"slab": me_s - 1}),
        (has_right, {"slab": me_s + 1}),
        (has_prev, {"energy": me_e - 1}),
        (has_next, {"energy": me_e + 1}),
    )
    for there, device in sides:
        @pl.when(there)
        def _(device=device):
            pl.semaphore_signal(barrier, inc=1, device_id=device, device_id_type=MESH)
    peers = sum(there.astype(jnp.int32) for there, _ in sides)
    pl.semaphore_wait(barrier, peers)

    def slab_copy(r, e, direction):
        halo = wide[r][e]
        if direction == 0:
            src, dst, to = green.at[e, atoms - HALO : atoms, r], halo.at[0:HALO], me_s + 1
        else:
            src, dst, to = green.at[e, 0:HALO, r], halo.at[HALO + atoms : 2 * HALO + atoms], me_s - 1
        return pltpu.make_async_remote_copy(
            src_ref=src,
            dst_ref=dst,
            send_sem=slab_send.at[direction, r, e],
            recv_sem=slab_recv.at[direction, r, e],
            device_id={"slab": to},
            device_id_type=MESH,
        )

    for r in range(parts):
        for e in order:
            @pl.when(has_right)
            def _(e=e, r=r):
                slab_copy(r, e, 0).start()
            @pl.when(has_left)
            def _(e=e, r=r):
                slab_copy(r, e, 1).start()

    def energy_copy(r, u, direction):
        if direction == 0:
            src, dst, to = low_send.at[r, u], low_recv.at[r, u], me_e + 1
        else:
            src, dst, to = up_send.at[r, u], up_recv.at[r, u], me_e - 1
        return pltpu.make_async_remote_copy(
            src_ref=src,
            dst_ref=dst,
            send_sem=en_send.at[direction, r, u],
            recv_sem=en_recv.at[direction, r, u],
            device_id={"energy": to},
            device_id_type=MESH,
        )

    @pl.when(jnp.logical_not(has_prev))
    def _():
        low_recv[...] = jnp.zeros_like(low_recv)
    @pl.when(jnp.logical_not(has_next))
    def _():
        up_recv[...] = jnp.zeros_like(up_recv)

    first_atom = me_s * atoms

    def products(r, e):
        def body(a, carry):
            halves, mats = [], []
            for j in range(slots):
                g = wide[r][e][jnp.clip(nbr[a, j] - first_atom + HALO, 0, atoms + 2 * HALO - 1)]
                c = coup[a, j]
                mats.append(c)
                h = jnp.dot(c.reshape(modes * blk, blk), g, preferred_element_type=jnp.float32)
                halves.append(h.astype(jnp.bfloat16))
            for m in range(modes):
                lhs = jnp.concatenate([h[m * blk : (m + 1) * blk] for h in halves], axis=1)
                rhs = jnp.concatenate([c[m] for c in mats], axis=1)
                p = lax.dot_general(lhs, rhs, (((1,), (1,)), ((), ())), preferred_element_type=jnp.float32)
                prod[m, r, e, a] = p.astype(jnp.bfloat16)
            return carry

        lax.fori_loop(0, atoms, body, 0)

    def store_sum(target, r, u, terms):
        def body(a, carry):
            total = None
            for m, index, weight in terms:
                inside = (index >= 0) & (index < energies)
                safe = jnp.clip(index, 0, energies - 1)
                term = jnp.where(inside, weight, 0.0) * prod[m, r, safe, a].astype(jnp.float32)
                total = term if total is None else total + term
            target[r, u, a] = total.astype(target.dtype)
            return carry

        lax.fori_loop(0, atoms, body, 0)

    for r in range(parts):
        done, sent = set(), set()
        for e in order:
            local[r][e].wait()
            if r == 0 and not done:
                coup_copy.wait()
                for copy in small:
                    copy.wait()
            @pl.when(has_left)
            def _(e=e, r=r):
                slab_copy(r, e, 0).wait_recv()
            @pl.when(has_right)
            def _(e=e, r=r):
                slab_copy(r, e, 1).wait_recv()
            products(r, e)
            done.add(e)
            for u in range(WID):
                if ("up", u) not in sent and set(range(u + 1)) <= done:
                    sent.add(("up", u))
                    @pl.when(has_prev)
                    def _(u=u, r=r):
                        store_sum(up_send, r, u, [(m, u - WID + shifts[m], occ[m]) for m in range(modes)])
                        energy_copy(r, u, 1).start()
            for u in reversed(range(WID)):
                if ("low", u) not in sent and set(range(energies - WID + u, energies)) <= done:
                    sent.add(("low", u))
                    @pl.when(has_next)
                    def _(u=u, r=r):
                        store_sum(
                            low_send, r, u, [(m, energies + u - shifts[m], occ[m] + 1.0) for m in range(modes)]
                        )
                        energy_copy(r, u, 0).start()

    for r in range(parts):
        for t in range(energies):
            terms = []
            for m in range(modes):
                terms.append((m, t - shifts[m], occ[m] + 1.0))
                terms.append((m, t + shifts[m], occ[m]))
            store_sum(own, r, t, terms)

    for r in range(parts):
        for t in reversed(order):
            low_u = t if t < WID else None
            up_u = t - (energies - WID) if t >= energies - WID else None
            if low_u is not None:
                @pl.when(has_prev)
                def _(u=low_u, r=r):
                    energy_copy(r, u, 0).wait_recv()
            if up_u is not None:
                @pl.when(has_next)
                def _(u=up_u, r=r):
                    energy_copy(r, u, 1).wait_recv()

            def body(a, carry, t=t, r=r, low_u=low_u, up_u=up_u):
                total = own[r, t, a]
                if low_u is not None:
                    total = total + low_recv[r, low_u, a].astype(jnp.float32)
                if up_u is not None:
                    total = total + up_recv[r, up_u, a].astype(jnp.float32)
                out[t, a, r] = total.astype(jnp.bfloat16)
                return carry

            lax.fori_loop(0, atoms, body, 0)

    for r in range(parts):
        for e in order:
            @pl.when(has_right)
            def _(e=e, r=r):
                slab_copy(r, e, 0).wait_send()
            @pl.when(has_left)
            def _(e=e, r=r):
                slab_copy(r, e, 1).wait_send()
        for u in range(WID):
            @pl.when(has_next)
            def _(u=u, r=r):
                energy_copy(r, u, 0).wait_send()
            @pl.when(has_prev)
            def _(u=u, r=r):
                energy_copy(r, u, 1).wait_send()


def solution(mesh):
    def shards(green, coupling, neighbours, shifts, occupation):
        energies, atoms, parts, blk, _ = green.shape
        slots, modes = coupling.shape[1:3]
        sizes = (energies, atoms, parts, blk, slots, modes, mesh.shape["energy"], mesh.shape["slab"])
        bf16, f32 = jnp.bfloat16, jnp.float32
        hbm = pl.BlockSpec(memory_space=pltpu.HBM)
        edge = (parts, WID, atoms, blk, blk)
        dma = pltpu.SemaphoreType.DMA
        return pl.pallas_call(
            functools.partial(kernel, sizes),
            out_shape=pltpu.VMEM(green.shape, bf16),
            in_specs=[hbm] * 5,
            out_specs=pl.BlockSpec(memory_space=pltpu.VMEM),
            scratch_shapes=[pltpu.VMEM((atoms + 2 * HALO, blk, blk), bf16) for _ in range(parts * energies)]
            + [
                pltpu.VMEM(coupling.shape, bf16),
                pltpu.VMEM((modes, parts, energies, atoms, blk, blk), bf16),
                pltpu.VMEM(edge, bf16),
                pltpu.VMEM(edge, bf16),
                pltpu.VMEM(edge, bf16),
                pltpu.VMEM(edge, bf16),
                pltpu.VMEM((parts, energies, atoms, blk, blk), f32),
                pltpu.SMEM((atoms, slots), jnp.int32),
                pltpu.SMEM((modes,), jnp.int32),
                pltpu.SMEM((modes,), f32),
                dma,
                dma((parts, energies)),
                dma((2, parts, energies)),
                dma((2, parts, energies)),
                dma((2, parts, WID)),
                dma((2, parts, WID)),
                dma((3,)),
            ],
            compiler_params=pltpu.CompilerParams(collective_id=0, has_side_effects=True),
        )(neighbours, shifts, occupation, green, coupling)

    return jax.shard_map(
        shards,
        mesh=mesh,
        in_specs=(
            P("energy", "slab", None, None, None),
            P("slab", None, None, None, None),
            P("slab", None),
            P(),
            P(),
        ),
        out_specs=P("energy", "slab", None, None, None),
        check_vma=False,
    )
```
